32 devices in a mesh: blk: 4 (over y, core), layer: 4 (over z), shard: 2 (over x).
Axes of the slice: x: 2, y: 2, z: 4, core: 2. Of those that a mesh axis runs over, the one named last changes fastest.
Arguments:
- train_grads: bfloat16 [8192, 4, 4096], P(('blk', 'shard'), 'layer'), may hold values from -6 to 6
- query_grads: bfloat16 [256, 4, 4096], P(('blk', 'shard'), 'layer'), may hold values from -6 to 6
- in_factor: bfloat16 [4, 64, 64], P('layer'), as said below
- out_factor: bfloat16 [4, 64, 64], P('layer'), as said below
Outputs:
- scores: float32 [256, 8192], P('layer', ('blk', 'shard'))
The draws below stay inside these ranges and needn't reach their ends.
Inputs may be any that keep to these rules, and one draw needn't show every extreme that they name: `in_factor`: Symmetric, with a dominant positive diagonal. `out_factor`: Symmetric, with a dominant positive diagonal.
All inputs are finite; a program needn't handle non-finite values.
Results may differ from the reference program's by a relative error of at most 0.012.
Values may be sent and summed in bfloat16 or wider, within the bound.
A program may use at most 64 MiB of HBM per device.

```python
import jax
import jax.numpy as jnp
from jax import lax

PROJ = 64
GRAD = 4096
LAYERS = 4
NTRAIN = 8192
NQUERY = 256


def factor_matrix(key, salt):
    inner = jax.random.fold_in(key, salt)
    first, second = jax.random.split(inner)
    diag = jax.random.uniform(first, (LAYERS, PROJ), jnp.float32, 1.0, 2.0)
    noise = jax.random.normal(second, (LAYERS, PROJ, PROJ), jnp.float32) * 0.06
    mirror = (noise + jnp.swapaxes(noise, 1, 2)) / jnp.sqrt(2.0)
    eye = jnp.eye(PROJ, dtype=jnp.float32)
    return (mirror * (1.0 - eye) + eye * diag[:, :, None]).astype(jnp.bfloat16)


def draw_in_factor(key, part):
    return factor_matrix(key, 11)


def draw_out_factor(key, part):
    return factor_matrix(key, 23)


def strengthened(array, rng, source, target, parts, factor):
    owner, partner = [(jnp.arange(array.shape[position]) // (array.shape[position] // parts)).reshape([-1 if axis == position else 1 for axis in range(array.ndim)]) for position in (source, target)]
    chosen = jax.random.permutation(rng, parts)[partner]
    strong = (owner == chosen) | (owner == (partner + parts // 2) % parts)
    return jnp.where(strong, factor * array, array)


def block_scale(stream_key, dims, cuts, least, largest):
    loudness, own = 1.0, jax.random.fold_in(stream_key, 6)
    for position, shards_of in cuts:
        steps = jnp.exp(jax.random.uniform(jax.random.fold_in(own, position), (shards_of,), jnp.float32, least / len(cuts), largest / len(cuts)))
        loudness = loudness * jnp.repeat(steps, dims[position] // shards_of).reshape([-1 if axis == position else 1 for axis in range(len(dims))])
    return loudness


def scatter_about(key, shape, spread, reach, pieces=(), kind=jnp.bfloat16):
    entries = jax.random.normal(key, shape, jnp.float32) * spread
    if len(pieces) > 0:
        entries = block_scale(key, shape, pieces, -0.22, 0.18) * entries
    return jnp.clip(entries, min=-reach, max=reach).astype(kind)


def heavy_noise(own_key, extent, width, most, shards, heavy, kind=jnp.bfloat16):
    array = width * jax.random.normal(own_key, extent, jnp.float32)
    if shards:
        array = array * block_scale(own_key, extent, shards, -0.22, 0.18)
    return jnp.clip(strengthened(array, jax.random.fold_in(own_key, 3), *heavy), -most, most).astype(kind)


def setup_inputs(seed: int = 0) -> dict:
    key_of = jax.random.split(jax.random.key(seed), 5)
    train_grads = scatter_about(key_of[0], (NTRAIN, LAYERS, GRAD), 1.0, 6.0, ((0, 8), (1, 4)))
    query_grads = heavy_noise(key_of[1], (NQUERY, LAYERS, GRAD), 1.0, 6.0, ((0, 8), (1, 4)), (1, 0, 4, 2.0))
    in_factor = draw_in_factor(jax.random.fold_in(key_of[4], 71), 0)
    out_factor = draw_out_factor(jax.random.fold_in(key_of[4], 71), 0)
    return {"train_grads": train_grads, "query_grads": query_grads, "in_factor": in_factor, "out_factor": out_factor}


score_scale = 1.0 / 128.0


def precondition(rows, inward, outward):
    count = rows.shape[0]
    cube = rows.reshape(count, PROJ, PROJ).astype(jnp.float32)
    half = jnp.einsum("nio,op->nip", cube, outward.astype(jnp.float32)).astype(jnp.bfloat16)
    half = lax.optimization_barrier(half)
    ready = jnp.einsum("ji,nip->njp", inward.astype(jnp.float32), half.astype(jnp.float32)).astype(jnp.bfloat16)
    return ready.reshape(count, GRAD)


def reference(train_grads, query_grads, in_factor, out_factor):
    total = jnp.zeros((NQUERY, NTRAIN), jnp.float32)
    for level in range(LAYERS):
        ready = precondition(query_grads[:, level, :], in_factor[level], out_factor[level])
        term = jnp.dot(ready, train_grads[:, level, :].T, preferred_element_type=jnp.float32) * score_scale
        term = lax.optimization_barrier(term.astype(jnp.bfloat16))
        total = total + term.astype(jnp.float32)
    return total
```

```python
import functools

import jax
import jax.numpy as jnp
from jax import lax
from jax.experimental import pallas as pl
from jax.experimental.pallas import tpu as pltpu
from jax.sharding import PartitionSpec as P

MESH = pl.DeviceIdType.MESH
score_scale = 1.0 / 128.0
bf16 = jnp.bfloat16
f32 = jnp.float32


def dot(a, b):
    return jnp.dot(a, b, preferred_element_type=f32)


def where_eq(shape, row_of, col_of):
    rows = lax.broadcasted_iota(jnp.int32, shape, 0)
    cols = lax.broadcasted_iota(jnp.int32, shape, 1)
    return (row_of(rows) == col_of(cols)).astype(f32).astype(bf16)


def precondition(query, inward, outward, spread, packed, own):
    rows, grad = query.shape
    proj = inward.shape[0]
    pair = proj // 2
    lanes = 2 * proj
    same = lambda v: v
    low = where_eq((proj, lanes), same, same)
    high = where_eq((proj, lanes), lambda r: r + proj, same)
    o_low = dot(outward, low)
    o_high = dot(outward, high)
    weight = jnp.concatenate(
        [jnp.concatenate([o_low, o_high], axis=1), jnp.concatenate([o_high, o_low], axis=1)], axis=0
    ).astype(bf16)
    stacked = jnp.concatenate([query[:, c * lanes : (c + 1) * lanes] for c in range(pair)], axis=0)
    half = dot(stacked, weight)
    for c in range(pair):
        part = half[c * rows : (c + 1) * rows]
        spread[pl.ds(c, rows, stride=proj), :] = part[:, :lanes]
        spread[pl.ds(pair + c, rows, stride=proj), :] = part[:, lanes:]
    split = where_eq((proj, proj), lambda r: 2 * (r % pair) + r // pair, same)
    ordered = dot(split, inward).astype(bf16)
    straight = where_eq((proj, proj), same, lambda k: 2 * (k % pair) + k // pair)
    crossed = where_eq((proj, proj), same, lambda k: 2 * (k % pair) + 1 - k // pair)
    row_id = lax.broadcasted_iota(jnp.int32, (proj, proj), 0)
    mixed = jnp.where(row_id < pair, dot(ordered, straight), dot(ordered, crossed)).astype(bf16)
    lane_id = lax.broadcasted_iota(jnp.int32, (pair, 2 * lanes), 1)
    for n in range(0, rows, 2):
        two = jnp.concatenate(
            [spread[pl.ds(n * proj, proj), :], spread[pl.ds((n + 1) * proj, proj), :]], axis=1
        ).astype(bf16)
        full = dot(mixed, two)
        ready = jnp.where(lane_id % lanes < proj, full[:pair], full[pair:])
        packed[pl.ds(n * pair, pair), :] = ready[:, :lanes]
        packed[pl.ds((n + 1) * pair, pair), :] = ready[:, lanes:]
    for d in range(pair):
        chunk = packed[pl.ds(d, rows, stride=pair), :].astype(bf16)
        own[0, :, d * lanes : (d + 1) * lanes] = chunk[: rows // 2]
        own[1, :, d * lanes : (d + 1) * lanes] = chunk[rows // 2 :]


def kernel(
    sizes,
    train_hbm,
    query_hbm,
    in_hbm,
    out_hbm,
    scores,
    train,
    query,
    inward,
    outward,
    spread,
    packed,
    pieces,
    terms,
    landed,
    load_sem,
    small_sem,
    send_sem,
    arrive,
    crossed,
    term_send,
    term_recv,
):
    n_blk, n_layer, n_shard = sizes
    n_core = 2 if n_blk % 2 == 0 else 1
    n_y = n_blk // n_core
    blk, layer, s = lax.axis_index("blk"), lax.axis_index("layer"), lax.axis_index("shard")
    y, c = blk // n_core, blk % n_core
    per_owner = n_blk * n_shard // n_layer
    tile = train.shape[1]

    y_at = lambda dy: lax.rem(y + dy, n_y)
    s_at = lambda ds: lax.rem(s + ds, n_shard)
    l_at = lambda dl: lax.rem(layer + dl, n_layer)
    blk_of = lambda yy, cc: yy * n_core + cc
    piece_of = lambda yy, cc, ss: blk_of(yy, cc) * n_shard + ss
    to_s = lambda ds: {"blk": blk, "layer": layer, "shard": s_at(ds)}
    to_y = lambda dy: {"blk": blk_of(y_at(dy), c), "layer": layer, "shard": s}
    to_core = {"blk": blk_of(y, 1 - c), "layer": layer, "shard": s}
    to_l = lambda ll: {"blk": blk, "layer": ll, "shard": s}

    barrier = pltpu.get_barrier_semaphore()
    friends = [to_s(ds) for ds in range(1, n_shard)] + [to_y(dy) for dy in range(1, n_y)]
    friends += [to_core] * (n_core - 1) + [to_l(l_at(dl)) for dl in range(1, n_layer)]
    for friend in friends:
        pl.semaphore_signal(barrier, inc=1, device_id=friend, device_id_type=MESH)

    smalls = [
        pltpu.make_async_copy(query_hbm, query, small_sem.at[0]),
        pltpu.make_async_copy(in_hbm, inward, small_sem.at[1]),
        pltpu.make_async_copy(out_hbm, outward, small_sem.at[2]),
    ]
    for copy in smalls:
        copy.start()
    loads = [
        pltpu.make_async_copy(train_hbm.at[pl.ds(t * tile, tile)], train.at[t], load_sem.at[t])
        for t in range(train.shape[0])
    ]
    for copy in loads:
        copy.start()
    for copy in smalls:
        copy.wait()

    mine = piece_of(y, c, s)
    precondition(query[...], inward[...], outward[...], spread, packed, pieces.at[mine])

    pl.semaphore_wait(barrier, len(friends))

    sent = []

    def send(index, h, sems, yy, ss, device):
        copy = pltpu.make_async_remote_copy(
            src_ref=pieces.at[index, h],
            dst_ref=pieces.at[index, h],
            send_sem=send_sem.at[len(sent)],
            recv_sem=sems.at[yy, ss, h],
            device_id=device,
            device_id_type=MESH,
        )
        copy.start()
        sent.append(copy)

    def wait(index, h, sems, yy, ss):
        pltpu.make_async_remote_copy(
            src_ref=pieces.at[index, h],
            dst_ref=pieces.at[index, h],
            send_sem=send_sem.at[0],
            recv_sem=sems.at[yy, ss, h],
            device_id=to_core,
            device_id_type=MESH,
        ).wait_recv()

    def pass_on(yy, ss, h):
        if n_core > 1:
            send(piece_of(yy, c, ss), h, crossed, yy, ss, to_core)

    def take(yy, ss, h):
        wait(piece_of(yy, c, ss), h, arrive, yy, ss)

    for h in range(2):
        pass_on(y, s, h)
    for h in range(2):
        for ds in range(1, n_shard):
            send(mine, h, arrive, y, s, to_s(ds))
        for dy in range(1, n_y):
            send(mine, 1 - h, arrive, y, s, to_y(dy))

    term_copies = []

    def term_copy(g):
        owner = g // per_owner
        return owner, pltpu.make_async_remote_copy(
            src_ref=terms.at[g],
            dst_ref=landed.at[layer, g % per_owner],
            send_sem=term_send.at[g],
            recv_sem=term_recv.at[layer, g % per_owner],
            device_id=to_l(owner),
            device_id_type=MESH,
        )

    def multiply(yy, ss):
        for other in range(1, n_core):
            for h in range(2):
                wait(piece_of(yy, 1 - c, ss), h, crossed, yy, ss)
        index = [piece_of(yy, cc, ss) for cc in range(n_core)]
        rows = query.shape[0]
        left = jnp.concatenate([pieces[g].reshape(rows, query.shape[1]) for g in index], axis=0)
        for t in range(train.shape[0]):
            if not term_copies:
                loads[t].wait()
            term = lax.dot_general(
                left, train[t], (((1,), (1,)), ((), ())), preferred_element_type=f32
            )
            term = (term * score_scale).astype(bf16)
            for k, g in enumerate(index):
                terms[g, :, t * tile : (t + 1) * tile] = term[k * rows : (k + 1) * rows]
        for g in index:
            owner, copy = term_copy(g)
            term_copies.append((owner, copy))

            @pl.when(owner != layer)
            def _():
                copy.start()

    multiply(y, s)
    for ds in range(1, n_shard):
        take(y, s_at(ds), 0)
        for dy in range(1, n_y):
            send(piece_of(y, c, s_at(ds)), 0, arrive, y, s_at(ds), to_y(dy))
        pass_on(y, s_at(ds), 0)
    for dy in range(1, n_y):
        take(y_at(dy), s, 1)
        for ds in range(1, n_shard):
            send(piece_of(y_at(dy), c, s), 1, arrive, y_at(dy), s, to_s(ds))
        pass_on(y_at(dy), s, 1)
    for ds in range(1, n_shard):
        take(y, s_at(ds), 1)
        pass_on(y, s_at(ds), 1)
    for dy in range(1, n_y):
        take(y_at(dy), s, 0)
        pass_on(y_at(dy), s, 0)
    for ds in range(1, n_shard):
        multiply(y, s_at(ds))
    for dy in range(1, n_y):
        for ds in range(1, n_shard):
            for h in range(2):
                take(y_at(dy), s_at(ds), h)
                pass_on(y_at(dy), s_at(ds), h)
    for dy in range(1, n_y):
        multiply(y_at(dy), s)
    for dy in range(1, n_y):
        for ds in range(1, n_shard):
            multiply(y_at(dy), s_at(ds))

    rows = query.shape[0]
    for j in range(per_owner):
        total = terms[layer * per_owner + j].astype(f32)
        for dl in range(1, n_layer):
            ll = l_at(dl)
            pltpu.make_async_remote_copy(
                src_ref=terms.at[0],
                dst_ref=landed.at[ll, j],
                send_sem=term_send.at[0],
                recv_sem=term_recv.at[ll, j],
                device_id=to_l(ll),
                device_id_type=MESH,
            ).wait_recv()
            total = total + landed[ll, j].astype(f32)
        scores[j * rows : (j + 1) * rows, :] = total

    for copy in sent:
        copy.wait_send()
    for owner, copy in term_copies:

        @pl.when(owner != layer)
        def _():
            copy.wait_send()


def solution(mesh):
    n_blk, n_layer, n_shard = mesh.shape["blk"], mesh.shape["layer"], mesh.shape["shard"]
    n_core = 2 if n_blk % 2 == 0 else 1
    n_y = n_blk // n_core

    def per_device(train_grads, query_grads, in_factor, out_factor):
        train_rows = train_grads[:, 0, :]
        panel = query_grads[:, 0, :]
        inward = in_factor[0]
        outward = out_factor[0]
        count, grad = train_rows.shape
        rows = panel.shape[0]
        proj = inward.shape[0]
        total = n_blk * n_shard
        per_owner = total // n_layer
        tiles = 4
        relay = 2 * (n_y - 1) * (n_shard - 1)
        sends = 2 * (n_y - 1 + n_shard - 1) + relay + 2 * n_y * n_shard * (n_core - 1)
        dma = pltpu.SemaphoreType.DMA
        return pl.pallas_call(
            functools.partial(kernel, (n_blk, n_layer, n_shard)),
            out_shape=jax.ShapeDtypeStruct((rows * per_owner, count), f32),
            in_specs=[pl.BlockSpec(memory_space=pl.ANY)] * 4,
            out_specs=pl.BlockSpec(memory_space=pltpu.VMEM),
            scratch_shapes=[
                pltpu.VMEM((tiles, count // tiles, grad), bf16),
                pltpu.VMEM((rows, grad), bf16),
                pltpu.VMEM((proj, proj), bf16),
                pltpu.VMEM((proj, proj), bf16),
                pltpu.VMEM((rows * proj, 2 * proj), f32),
                pltpu.VMEM((rows * proj // 2, 2 * proj), f32),
                pltpu.VMEM((total, 2, rows // 2, grad), bf16),
                pltpu.VMEM((total, rows, count), bf16),
                pltpu.VMEM((n_layer, per_owner, rows, count), bf16),
                dma((tiles,)),
                dma((3,)),
                dma((sends,)),
                dma((n_y, n_shard, 2)),
                dma((n_y, n_shard, 2)),
                dma((total,)),
                dma((n_layer, per_owner)),
            ],
            compiler_params=pltpu.CompilerParams(
                collective_id=0, has_side_effects=True, vmem_limit_bytes=56 * 1024 * 1024
            ),
        )(train_rows, panel, inward, outward)

    in_specs = (
        P(("blk", "shard"), "layer", None),
        P(("blk", "shard"), "layer", None),
        P("layer", None, None),
        P("layer", None, None),
    )
    out_specs = P("layer", ("blk", "shard"))
    return jax.shard_map(
        per_device, mesh=mesh, in_specs=in_specs, out_specs=out_specs, check_vma=False
    )
```

```python
import functools

import jax
import jax.numpy as jnp
from jax import lax
from jax.experimental import pallas as pl
from jax.experimental.pallas import tpu as pltpu
from jax.sharding import PartitionSpec as P

MESH = pl.DeviceIdType.MESH
score_scale = 1.0 / 128.0
bf16 = jnp.bfloat16
f32 = jnp.float32


def dot(a, b):
    return jnp.dot(a, b, preferred_element_type=f32)


def where_eq(shape, row_of, col_of):
    rows = lax.broadcasted_iota(jnp.int32, shape, 0)
    cols = lax.broadcasted_iota(jnp.int32, shape, 1)
    return (row_of(rows) == col_of(cols)).astype(f32).astype(bf16)


def precondition(query, inward, outward, spread, packed, own):
    rows, grad = query.shape
    proj = inward.shape[0]
    pair = proj // 2
    lanes = 2 * proj
    same = lambda v: v
    low = where_eq((proj, lanes), same, same)
    high = where_eq((proj, lanes), lambda r: r + proj, same)
    o_low = dot(outward, low)
    o_high = dot(outward, high)
    weight = jnp.concatenate(
        [jnp.concatenate([o_low, o_high], axis=1), jnp.concatenate([o_high, o_low], axis=1)], axis=0
    ).astype(bf16)
    stacked = jnp.concatenate([query[:, c * lanes : (c + 1) * lanes] for c in range(pair)], axis=0)
    half = dot(stacked, weight)
    for c in range(pair):
        part = half[c * rows : (c + 1) * rows]
        spread[pl.ds(c, rows, stride=proj), :] = part[:, :lanes]
        spread[pl.ds(pair + c, rows, stride=proj), :] = part[:, lanes:]
    split = where_eq((proj, proj), lambda r: 2 * (r % pair) + r // pair, same)
    ordered = dot(split, inward).astype(bf16)
    straight = where_eq((proj, proj), same, lambda k: 2 * (k % pair) + k // pair)
    crossed = where_eq((proj, proj), same, lambda k: 2 * (k % pair) + 1 - k // pair)
    row_id = lax.broadcasted_iota(jnp.int32, (proj, proj), 0)
    mixed = jnp.where(row_id < pair, dot(ordered, straight), dot(ordered, crossed)).astype(bf16)
    lane_id = lax.broadcasted_iota(jnp.int32, (pair, 2 * lanes), 1)
    for n in range(0, rows, 2):
        two = jnp.concatenate(
            [spread[pl.ds(n * proj, proj), :], spread[pl.ds((n + 1) * proj, proj), :]], axis=1
        ).astype(bf16)
        full = dot(mixed, two)
        ready = jnp.where(lane_id % lanes < proj, full[:pair], full[pair:])
        packed[pl.ds(n * pair, pair), :] = ready[:, :lanes]
        packed[pl.ds((n + 1) * pair, pair), :] = ready[:, lanes:]
    for d in range(pair):
        chunk = packed[pl.ds(d, rows, stride=pair), :].astype(bf16)
        own[0, :, d * lanes : (d + 1) * lanes] = chunk[: rows // 2]
        own[1, :, d * lanes : (d + 1) * lanes] = chunk[rows // 2 :]


def kernel(
    sizes,
    train_hbm,
    query_hbm,
    in_hbm,
    out_hbm,
    scores,
    train,
    query,
    inward,
    outward,
    spread,
    packed,
    pieces,
    terms,
    landed,
    gated,
    load_sem,
    small_sem,
    send_sem,
    arrive,
    crossed,
    term_send,
    term_recv,
    gate_recv,
):
    n_blk, n_layer, n_shard = sizes
    n_core = 2 if n_blk % 2 == 0 else 1
    n_y = n_blk // n_core
    blk, layer, s = lax.axis_index("blk"), lax.axis_index("layer"), lax.axis_index("shard")
    y, c = blk // n_core, blk % n_core
    per_owner = n_blk * n_shard // n_layer
    tile = train.shape[1]

    y_at = lambda dy: lax.rem(y + dy, n_y)
    s_at = lambda ds: lax.rem(s + ds, n_shard)
    l_at = lambda dl: lax.rem(layer + dl, n_layer)
    blk_of = lambda yy, cc: yy * n_core + cc
    piece_of = lambda yy, cc, ss: blk_of(yy, cc) * n_shard + ss
    to_s = lambda ds: {"blk": blk, "layer": layer, "shard": s_at(ds)}
    to_y = lambda dy: {"blk": blk_of(y_at(dy), c), "layer": layer, "shard": s}
    to_core = {"blk": blk_of(y, 1 - c), "layer": layer, "shard": s}
    to_l = lambda ll: {"blk": blk, "layer": ll, "shard": s}

    barrier = pltpu.get_barrier_semaphore()
    friends = [to_s(ds) for ds in range(1, n_shard)] + [to_y(dy) for dy in range(1, n_y)]
    friends += [to_core] * (n_core - 1) + [to_l(l_at(dl)) for dl in range(1, n_layer)]
    for friend in friends:
        pl.semaphore_signal(barrier, inc=1, device_id=friend, device_id_type=MESH)

    smalls = [
        pltpu.make_async_copy(query_hbm, query, small_sem.at[0]),
        pltpu.make_async_copy(in_hbm, inward, small_sem.at[1]),
        pltpu.make_async_copy(out_hbm, outward, small_sem.at[2]),
    ]
    for copy in smalls:
        copy.start()
    loads = [
        pltpu.make_async_copy(train_hbm.at[pl.ds(t * tile, tile)], train.at[t], load_sem.at[t])
        for t in range(train.shape[0])
    ]
    for copy in loads:
        copy.start()
    for copy in smalls:
        copy.wait()

    mine = piece_of(y, c, s)
    precondition(query[...], inward[...], outward[...], spread, packed, pieces.at[mine])

    pl.semaphore_wait(barrier, len(friends))

    sent = []

    def send(index, h, sems, yy, ss, device):
        copy = pltpu.make_async_remote_copy(
            src_ref=pieces.at[index, h],
            dst_ref=pieces.at[index, h],
            send_sem=send_sem.at[len(sent)],
            recv_sem=sems.at[yy, ss, h],
            device_id=device,
            device_id_type=MESH,
        )
        copy.start()
        sent.append(copy)

    def wait(index, h, sems, yy, ss):
        pltpu.make_async_remote_copy(
            src_ref=pieces.at[index, h],
            dst_ref=pieces.at[index, h],
            send_sem=send_sem.at[0],
            recv_sem=sems.at[yy, ss, h],
            device_id=to_core,
            device_id_type=MESH,
        ).wait_recv()

    def pass_on(yy, ss, h):
        if n_core > 1:
            send(piece_of(yy, c, ss), h, crossed, yy, ss, to_core)

    def take(yy, ss, h):
        wait(piece_of(yy, c, ss), h, arrive, yy, ss)

    for h in range(2):
        pass_on(y, s, h)
    for h in range(2):
        for ds in range(1, n_shard):
            send(mine, h, arrive, y, s, to_s(ds))
        for dy in range(1, n_y):
            send(mine, 1 - h, arrive, y, s, to_y(dy))

    half_l = n_layer // 2
    side, place = layer // half_l, lax.rem(layer, half_l)
    gate_of = lambda which: half_l - 1 + which
    is_gate = layer == gate_of(side)
    term_sent = []

    def term_copy(g, dst, recv, ll):
        return pltpu.make_async_remote_copy(
            src_ref=terms.at[g],
            dst_ref=dst,
            send_sem=term_send.at[g],
            recv_sem=recv,
            device_id=to_l(ll),
            device_id_type=MESH,
        )

    def owner_copy(g, slot):
        j = lax.rem(g, per_owner)
        return term_copy(g, landed.at[slot, j], term_recv.at[slot, j], g // per_owner)

    def gate_copy(g, slot):
        return term_copy(g, gated.at[slot, g], gate_recv.at[slot, g], gate_of(side))

    loaded = []

    def multiply(*chips):
        for yy, ss in chips:
            for other in range(1, n_core):
                for h in range(2):
                    wait(piece_of(yy, 1 - c, ss), h, crossed, yy, ss)
        index = [piece_of(yy, cc, ss) for yy, ss in chips for cc in range(n_core)]
        rows = query.shape[0]
        left = jnp.concatenate([pieces[g].reshape(rows, query.shape[1]) for g in index], axis=0)
        for t in range(train.shape[0]):
            if len(loaded) < train.shape[0]:
                loads[t].wait()
                loaded.append(t)
            term = lax.dot_general(
                train[t], left, (((1,), (1,)), ((), ())), preferred_element_type=f32
            )
            term = (term * score_scale).T.astype(bf16)
            for k, g in enumerate(index):
                terms[g, :, t * tile : (t + 1) * tile] = term[k * rows : (k + 1) * rows]
        for g in index:
            owner = g // per_owner
            near = owner // half_l == side

            @pl.when(jnp.logical_and(near, owner != layer))
            def _():
                owner_copy(g, place).start()

            @pl.when(jnp.logical_and(jnp.logical_not(near), jnp.logical_not(is_gate)))
            def _():
                gate_copy(g, place).start()

        term_sent.extend(index)
        return index

    def gather_gate(index):
        for g in index:
            far = g // per_owner // half_l != side

            @pl.when(jnp.logical_and(far, is_gate))
            def _():
                total = terms[g].astype(f32)
                for step in range(1, half_l):
                    slot = lax.rem(place + step, half_l)
                    gate_copy(g, slot).wait_recv()
                    total = total + gated[slot, g].astype(f32)
                terms[g] = total.astype(bf16)
                owner_copy(g, half_l).start()

    first = multiply((y, s))
    for ds in range(1, n_shard):
        take(y, s_at(ds), 0)
        for dy in range(1, n_y):
            send(piece_of(y, c, s_at(ds)), 0, arrive, y, s_at(ds), to_y(dy))
        pass_on(y, s_at(ds), 0)
    for dy in range(1, n_y):
        take(y_at(dy), s, 1)
        for ds in range(1, n_shard):
            send(piece_of(y_at(dy), c, s), 1, arrive, y_at(dy), s, to_s(ds))
        pass_on(y_at(dy), s, 1)
    for ds in range(1, n_shard):
        take(y, s_at(ds), 1)
        pass_on(y, s_at(ds), 1)
    for dy in range(1, n_y):
        take(y_at(dy), s, 0)
        pass_on(y_at(dy), s, 0)
    gather_gate(first)
    beside = [(y, s_at(ds)) for ds in range(1, n_shard)] + [(y_at(dy), s) for dy in range(1, n_y)]
    across = [(y_at(dy), s_at(ds)) for dy in range(1, n_y) for ds in range(1, n_shard)]
    second = multiply(*beside) if beside else []
    for yy, ss in across:
        for h in range(2):
            take(yy, ss, h)
            pass_on(yy, ss, h)
    third = multiply(*across) if across else []
    gather_gate(second)
    gather_gate(third)

    rows = query.shape[0]
    for j in range(per_owner):
        g = layer * per_owner + j
        total = terms[g].astype(f32)
        for step in range(1, half_l + 1):
            slot = half_l if step == half_l else lax.rem(place + step, half_l)
            owner_copy(g, slot).wait_recv()
            total = total + landed[slot, j].astype(f32)
        scores[j * rows : (j + 1) * rows, :] = total

    for copy in sent:
        copy.wait_send()
    for g in term_sent:

        @pl.when(g // per_owner != layer)
        def _():
            owner_copy(g, 0).wait_send()


def solution(mesh):
    n_blk, n_layer, n_shard = mesh.shape["blk"], mesh.shape["layer"], mesh.shape["shard"]
    n_core = 2 if n_blk % 2 == 0 else 1
    n_y = n_blk // n_core

    def per_device(train_grads, query_grads, in_factor, out_factor):
        train_rows = train_grads[:, 0, :]
        panel = query_grads[:, 0, :]
        inward = in_factor[0]
        outward = out_factor[0]
        count, grad = train_rows.shape
        rows = panel.shape[0]
        proj = inward.shape[0]
        total = n_blk * n_shard
        per_owner = total // n_layer
        tiles = 2
        relay = 2 * (n_y - 1) * (n_shard - 1)
        sends = 2 * (n_y - 1 + n_shard - 1) + relay + 2 * n_y * n_shard * (n_core - 1)
        dma = pltpu.SemaphoreType.DMA
        return pl.pallas_call(
            functools.partial(kernel, (n_blk, n_layer, n_shard)),
            out_shape=jax.ShapeDtypeStruct((rows * per_owner, count), f32),
            in_specs=[pl.BlockSpec(memory_space=pl.ANY)] * 4,
            out_specs=pl.BlockSpec(memory_space=pltpu.VMEM),
            scratch_shapes=[
                pltpu.VMEM((tiles, count // tiles, grad), bf16),
                pltpu.VMEM((rows, grad), bf16),
                pltpu.VMEM((proj, proj), bf16),
                pltpu.VMEM((proj, proj), bf16),
                pltpu.VMEM((rows * proj, 2 * proj), f32),
                pltpu.VMEM((rows * proj // 2, 2 * proj), f32),
                pltpu.VMEM((total, 2, rows // 2, grad), bf16),
                pltpu.VMEM((total, rows, count), bf16),
                pltpu.VMEM((n_layer // 2 + 1, per_owner, rows, count), bf16),
                pltpu.VMEM((n_layer // 2, total, rows, count), bf16),
                dma((tiles,)),
                dma((3,)),
                dma((sends,)),
                dma((n_y, n_shard, 2)),
                dma((n_y, n_shard, 2)),
                dma((total,)),
                dma((n_layer // 2 + 1, per_owner)),
                dma((n_layer // 2, total)),
            ],
            compiler_params=pltpu.CompilerParams(
                collective_id=0, has_side_effects=True, vmem_limit_bytes=56 * 1024 * 1024
            ),
        )(train_rows, panel, inward, outward)

    in_specs = (
        P(("blk", "shard"), "layer", None),
        P(("blk", "shard"), "layer", None),
        P("layer", None, None),
        P("layer", None, None),
    )
    out_specs = P("layer", ("blk", "shard"))
    return jax.shard_map(
        per_device, mesh=mesh, in_specs=in_specs, out_specs=out_specs, check_vma=False
    )
```
